32 devices in a mesh: grow: 4 (over z), gy: 4 (over x, core), gz: 2 (over y).
Axes of the slice: x: 2, y: 2, z: 4, core: 2. Of those that a mesh axis runs over, the one named last changes fastest.
Arguments:
- labels: int32 [128, 32, 256], P('grow', 'gy', 'gz'), may hold values from 0 to 3
- potential: float32 [2, 128, 32, 256], P(None, 'grow', 'gy', 'gz'), may hold values from -3 to 3
- melt_codes: int32 [16, 32, 256], P(None, 'gy', 'gz'), may hold values from 0 to 7
- melt_table: float32 [2, 8], replicated, may hold values from -1 to 1
Outputs:
- phases: float32 [4, 128, 32, 256], P(None, 'grow', 'gy', 'gz')
- potentials: float32 [2, 128, 32, 256], P(None, 'grow', 'gy', 'gz')
The draws below stay inside these ranges and needn't reach their ends.
All inputs are finite; a program needn't handle non-finite values.
Results may differ from the reference program's by a relative error of at most 0.0001.
Values sent between devices are 32-bit elements; how exact they have to be, the bound alone decides.
A program may use at most 64 MiB of HBM per device.

```python
import jax
import jax.numpy as jnp
from jax import lax

SHIFT = 16
LEVELS = 8
STEPS_BEFORE = 3
STEPS_AFTER = 2
NG = 128
NY = 32
NZ = 256


def plant(values, stream_key, smallest, largest):
    place = [jax.random.randint(jax.random.fold_in(stream_key, axis), (), 0, length) for axis, length in enumerate(values.shape)]
    longest = values.shape.index(max(values.shape))
    next_to = place[:longest] + [(place[longest] + 1) % values.shape[longest]] + place[longest + 1:]
    return values.at[tuple(place)].set(smallest).at[tuple(next_to)].set(largest)


def block_levels(own_key, shape, cuts, low, top_value):
    level = 1.0
    for position, parts in cuts:
        draws = jax.random.uniform(jax.random.fold_in(jax.random.fold_in(own_key, 6), position), (parts,), jnp.float32, low / len(cuts), top_value / len(cuts))
        level = level * jnp.repeat(jnp.exp(draws), shape[position] // parts).reshape((-1,) + (1,) * (len(shape) - 1 - position))
    return level


def scatter_about(stream_key, shape, scale, limit, cuts=(), held_as=jnp.bfloat16):
    entries = scale * jax.random.normal(stream_key, shape, jnp.float32)
    if cuts:
        entries = entries * block_levels(stream_key, shape, cuts, -0.22, 0.18)
    return jnp.clip(entries, -limit, limit).astype(held_as)


def setup_inputs(seed: int = 0) -> dict:
    keys = jax.random.split(jax.random.key(seed), 5)
    labels = plant(jax.random.randint(keys[0], (NG, NY, NZ), 0, 4), jax.random.fold_in(keys[0], 1), 0, 3).astype(jnp.int32)
    potential = scatter_about(keys[1], (2, NG, NY, NZ), 0.5, 3.0, ((1, 4), (2, 4), (3, 2)), jnp.float32)
    melt_codes = plant(jax.random.randint(keys[2], (SHIFT, NY, NZ), 0, LEVELS), jax.random.fold_in(keys[2], 1), 0, LEVELS - 1).astype(jnp.int32)
    melt_table = jnp.clip(jax.random.uniform(keys[3], (2, LEVELS), jnp.float32, -1.0, 1.0), -1.0, 1.0)
    return {"labels": labels, "potential": potential, "melt_codes": melt_codes, "melt_table": melt_table}


comp_table = ((0.8, 0.1), (0.1, 0.8), (0.1, 0.1), (0.35, 0.35))
free_energy = (-0.05, -0.05, -0.05, 0.0)
diffusivity = (0.05, 0.05, 0.05, 1.0)
grad_rate = 0.12
well_rate = 0.3
drive_rate = 0.5
diff_rate = 0.15


def laplacian(fields, grow_padded, side_padded):
    total = grow_padded[:, 2:] + grow_padded[:, :-2]
    total = total + (side_padded[:, :, 2:, 1:-1] + side_padded[:, :, :-2, 1:-1])
    total = total + (side_padded[:, :, 1:-1, 2:] + side_padded[:, :, 1:-1, :-2])
    return total - 6.0 * fields


def advance(fields, grow_padded, side_padded):
    phases = fields[:4]
    chem_pot = fields[4:]
    laplace = laplacian(fields, grow_padded, side_padded)
    comp = jnp.array(comp_table, jnp.float32)
    comp_first = comp[:, 0].reshape(4, 1, 1, 1)
    comp_second = comp[:, 1].reshape(4, 1, 1, 1)
    energy = jnp.array(free_energy, jnp.float32).reshape(4, 1, 1, 1)
    spread = jnp.array(diffusivity, jnp.float32).reshape(4, 1, 1, 1)
    grand_pot = energy - (chem_pot[0:1] * comp_first + chem_pot[1:2] * comp_second)
    squares = phases * phases
    others = jnp.sum(squares, axis=0, keepdims=True) - squares
    slope = 6.0 * phases * (1.0 - phases)
    increment = grad_rate * laplace[:4] - 2.0 * well_rate * phases * others - drive_rate * slope * grand_pot
    increment = increment - jnp.mean(increment, axis=0, keepdims=True)
    clipped = jnp.clip(phases + increment, 0.0, 1.0)
    new_phases = clipped / jnp.sum(clipped, axis=0, keepdims=True)
    change = new_phases * new_phases * (3.0 - 2.0 * new_phases) - phases * phases * (3.0 - 2.0 * phases)
    mobility = jnp.sum(phases * spread, axis=0, keepdims=True)
    release = jnp.concatenate([jnp.sum(change * comp_first, axis=0, keepdims=True), jnp.sum(change * comp_second, axis=0, keepdims=True)], axis=0)
    new_chem = chem_pot + diff_rate * mobility * laplace[4:] - release
    return jnp.concatenate([new_phases, new_chem], axis=0)


def pad_faces(fields):
    grow_padded = jnp.concatenate([fields[:, :1], fields, fields[:, -1:]], axis=1)
    side_padded = jnp.concatenate([fields[:, :, -1:], fields, fields[:, :, :1]], axis=2)
    side_padded = jnp.concatenate([side_padded[:, :, :, -1:], side_padded, side_padded[:, :, :, :1]], axis=3)
    return grow_padded, side_padded


def melt_planes(melt_codes, melt_table):
    levels = melt_table.shape[1]
    onehot = (melt_codes[None] == jnp.arange(levels, dtype=jnp.int32).reshape(levels, 1, 1, 1)).astype(jnp.float32)
    chem_pot = jnp.einsum("ik,kabc->iabc", melt_table.astype(jnp.float32), onehot, precision=lax.Precision.HIGHEST)
    liquid = (jnp.arange(4, dtype=jnp.int32) == 3).astype(jnp.float32).reshape(4, 1, 1, 1)
    phases = jnp.broadcast_to(liquid, (4,) + melt_codes.shape)
    return jnp.concatenate([phases, chem_pot], axis=0)


def reference(labels, potential, melt_codes, melt_table):
    phases = (labels[None] == jnp.arange(4, dtype=jnp.int32).reshape(4, 1, 1, 1)).astype(jnp.float32)
    fields = jnp.concatenate([phases, potential], axis=0)
    for iteration in range(STEPS_BEFORE):
        grow_padded, side_padded = pad_faces(fields)
        fields = advance(fields, grow_padded, side_padded)
    fields = jnp.concatenate([fields[:, SHIFT:], melt_planes(melt_codes, melt_table)], axis=1)
    for iteration in range(STEPS_AFTER):
        grow_padded, side_padded = pad_faces(fields)
        fields = advance(fields, grow_padded, side_padded)
    return fields[:4], fields[4:]
```

```python
import functools

import jax
import jax.numpy as jnp
from jax import lax
from jax.experimental import pallas as pl
from jax.experimental.pallas import tpu as pltpu
from jax.sharding import PartitionSpec as P

STEPS_BEFORE = 3
STEPS_AFTER = 2
STEPS = STEPS_BEFORE + STEPS_AFTER
HALF = 7
WIDE = 2 * HALF
MESH = pl.DeviceIdType.MESH


class Plan:
    def __init__(self, planes, rows, shift):
        self.planes, self.rows, self.shift = planes, rows, shift
        self.skip = (shift - STEPS) // 8 * 8
        self.own = planes - self.skip
        self.above = shift + STEPS
        self.upper = -(-self.above // 8) * 8
        self.deep = self.own + self.upper
        self.first = shift - self.skip
        self.start = self.first - STEPS + 1
        self.tiles = -(-(planes + 2 * (STEPS - 1)) // 8)
        self.tall = rows + 2 * STEPS
        self.slots = self.tall // 2


def gather_kernel(plan, mesh_shape, levels, lab, pot, codes, table, main, strip, lab_up, pot_up, pack, g_send, g_recv, y_send, y_recv, z_send, z_recv):
    g, y, z = lax.axis_index("grow"), lax.axis_index("gy"), lax.axis_index("gz")
    count_g, count_y, count_z = mesh_shape
    rows, own, tall = plan.rows, plan.own, plan.tall
    has_below, has_above = g > 0, g < count_g - 1
    y_up, y_down = lax.rem(y + 1, count_y), lax.rem(y + count_y - 1, count_y)
    z_other = lax.rem(z + 1, count_z)

    barrier = pltpu.get_barrier_semaphore()

    def greet(target):
        pl.semaphore_signal(barrier, inc=1, device_id=target, device_id_type=MESH)

    @pl.when(has_below)
    def _():
        greet((g - 1, y, z))

    @pl.when(has_above)
    def _():
        greet((g + 1, y, z))

    greet((g, y_up, z))
    greet((g, y_down, z))
    greet((g, y, z_other))
    pl.semaphore_wait(barrier, 3 + has_below.astype(jnp.int32) + has_above.astype(jnp.int32))

    def g_copy(i):
        size = plan.above * rows
        src = lab.at[pl.ds(0, size)] if i == 0 else pot.at[i - 1, pl.ds(0, size)]
        dst = lab_up if i == 0 else pot_up.at[i - 1]
        return pltpu.make_async_remote_copy(
            src_ref=src, dst_ref=dst, send_sem=g_send.at[i], recv_sem=g_recv.at[i],
            device_id=(g - 1, y, z), device_id_type=MESH)

    @pl.when(has_below)
    def _():
        for i in range(3):
            g_copy(i).start()

    def y_copy(slot, values, low, size, up):
        if up:
            src, dst, target = rows, 0, y_up
        else:
            src, dst, target = STEPS, STEPS + rows, y_down
        return pltpu.make_async_remote_copy(
            src_ref=main.at[values, pl.ds(src, STEPS), pl.ds(low, size)],
            dst_ref=main.at[values, pl.ds(dst, STEPS), pl.ds(low, size)],
            send_sem=y_send.at[slot], recv_sem=y_recv.at[slot],
            device_id=(g, target, z), device_id_type=MESH)

    def row_of(ref, i, row, begin, size):
        at = pl.ds(begin * rows + row, size, stride=rows)
        return ref[at].astype(jnp.float32) if i == 0 else ref[i - 1, at]

    own_copies = []
    for i in range(3):
        for row in range(rows):
            main[i, STEPS + row, 0:own] = row_of(lab if i == 0 else pot, i, row, plan.skip, own)
        for up in (True, False):
            copy = y_copy(2 * i + up, i, 0, own, up)
            copy.start()
            own_copies.append(copy)

    up_copies = []
    for i in range(3):
        @pl.when(has_above)
        def _(i=i):
            g_copy(i).wait_recv()
            for row in range(rows):
                main[i, STEPS + row, own : own + plan.above] = row_of(lab_up if i == 0 else pot_up, i, row, 0, plan.above)
                rest = plan.upper - plan.above
                if rest:
                    main[i, STEPS + row, own + plan.above : plan.deep] = jnp.zeros((rest, 128), jnp.float32)

        @pl.when(jnp.logical_not(has_above))
        def _(i=i):
            for row in range(rows):
                if i == 0:
                    main[0, STEPS + row, own : own + plan.shift] = jnp.full((plan.shift, 128), 3.0, jnp.float32)
                else:
                    code = codes[pl.ds(row, plan.shift, stride=rows)]
                    value = jnp.zeros((plan.shift, 128), jnp.float32)
                    for level in range(levels):
                        value = jnp.where(code == level, table[i - 1, level], value)
                    main[i, STEPS + row, own : own + plan.shift] = value
                left = plan.deep - own - plan.shift
                main[i, STEPS + row, own + plan.shift : plan.deep] = jnp.zeros((left, 128), jnp.float32)

        for up in (True, False):
            copy = y_copy(6 + 2 * i + up, i, own, plan.upper, up)
            copy.start()
            up_copies.append(copy)

    lane = lax.broadcasted_iota(jnp.int32, (plan.deep, 128), 1)
    z_copies = []
    for i in range(3):
        for copy in own_copies[2 * i : 2 * i + 2] + up_copies[2 * i : 2 * i + 2]:
            copy.wait_recv()
        for parity in range(2):
            packed = jnp.zeros((plan.deep, 128), jnp.float32)
            for slot in range(plan.slots):
                turned = pltpu.roll(main[i, 2 * slot + parity], WIDE * slot + HALF, 1)
                inside = (lane >= WIDE * slot) & (lane < WIDE * slot + WIDE)
                packed = jnp.where(inside, turned, packed)
            pack[i, parity] = packed
        copy = pltpu.make_async_remote_copy(
            src_ref=pack.at[i], dst_ref=strip.at[i], send_sem=z_send.at[i], recv_sem=z_recv.at[i],
            device_id=(g, y, z_other), device_id_type=MESH)
        copy.start()
        z_copies.append(copy)

    for copy in z_copies:
        copy.wait()
    for copy in own_copies + up_copies:
        copy.wait_send()

    @pl.when(has_below)
    def _():
        for i in range(3):
            g_copy(i).wait_send()


def cell_step(center, laplace):
    p, (m0, m1) = center[:4], center[4:]
    both = m0 + m1
    third = 0.3 * both + 0.15
    minus_w = (third + 2.1 * m0, third + 2.1 * m1, third, 1.05 * both)
    squares = [v * v for v in p]
    total = (squares[0] + squares[1]) + (squares[2] + squares[3])
    scaled = 0.6 * total
    raw = []
    for a in range(4):
        inner = (1.0 - p[a]) * minus_w[a] - (scaled - 0.6 * squares[a])
        raw.append(0.12 * laplace[a] + p[a] * inner)
    mean = 0.25 * ((raw[0] + raw[1]) + (raw[2] + raw[3]))
    held = [jnp.clip(p[a] + (raw[a] - mean), 0.0, 1.0) for a in range(4)]
    inverse = 1.0 / ((held[0] + held[1]) + (held[2] + held[3]))
    new = [v * inverse for v in held]
    change = [new[a] * new[a] * (3.0 - 2.0 * new[a]) - squares[a] * (3.0 - 2.0 * p[a]) for a in range(4)]
    shared = 0.1 * (change[0] + change[1] + change[2]) + 0.35 * change[3]
    mobility = 0.15 * (0.05 * (p[0] + p[1] + p[2]) + p[3])
    new0 = m0 + mobility * laplace[4] - (shared + 0.7 * change[0])
    new1 = m1 + mobility * laplace[5] - (shared + 0.7 * change[1])
    return new + [new0, new1]


def steps_kernel(plan, count_g, main0, strip0, phases, potentials, main_a, main_b, strip_a, strip_b):
    g = lax.axis_index("grow")
    is_first, is_last = g == 0, g == count_g - 1
    rows, tall, deep = plan.rows, plan.tall, plan.deep

    def unpack(source, target, index):
        label = source[(0,) + index]
        for a in range(4):
            target[(a,) + index] = jnp.where(label == float(a), 1.0, 0.0)
        for i in range(2):
            target[(4 + i,) + index] = source[(1 + i,) + index]

    def unpack_row(row, carry):
        unpack(main0, main_a, (row,))
        return carry

    lax.fori_loop(0, tall, unpack_row, 0)
    for parity in range(2):
        unpack(strip0, strip_a, (parity,))

    lane = lax.broadcasted_iota(jnp.int32, (8, 128), 1)
    place = lax.broadcasted_iota(jnp.int32, (8, 128), 0)
    at_left, at_right = lane == 0, lane == 127
    inner_left, inner_right = lane % WIDE == HALF - 1, lane % WIDE == HALF

    def grow_sides(ref, index, low, center, top, bottom):
        above = ref[index + (pl.ds(low + 1, 8), slice(None))]
        below = ref[index + (pl.ds(low - 1, 8), slice(None))]
        if top is not None and low <= top < low + 8:
            above = jnp.where((place == top - low) & is_last, center, above)
        if bottom is not None and low <= bottom < low + 8:
            below = jnp.where((place == bottom - low) & is_first, center, below)
        return above + below

    def main_tile(src, strips, row, low, top, bottom):
        slot, parity = row // 2, lax.rem(row, 2)
        turn = 128 - (WIDE * slot + HALF)
        center, laplace = [], []
        for f in range(6):
            v = src[f, row, pl.ds(low, 8), :]
            near = pltpu.roll(strips[f, parity, pl.ds(low, 8), :], turn, 1)
            right = pltpu.roll(jnp.where(at_left, near, v), 127, 1)
            left = pltpu.roll(jnp.where(at_right, near, v), 1, 1)
            total = grow_sides(src, (f, row), low, v, top, bottom)
            total = total + (src[f, row + 1, pl.ds(low, 8), :] + src[f, row - 1, pl.ds(low, 8), :])
            total = total + (right + left)
            center.append(v)
            laplace.append(total - 6.0 * v)
        return cell_step(center, laplace)

    def strip_tile(src, strips, parity, low, top, bottom):
        center, laplace = [], []
        for f in range(6):
            v = strips[f, parity, pl.ds(low, 8), :]
            edge = jnp.zeros((8, 128), jnp.float32)
            for slot in range(plan.slots):
                turned = pltpu.roll(src[f, 2 * slot + parity, pl.ds(low, 8), :], WIDE * slot + HALF, 1)
                edge = jnp.where((lane >= WIDE * slot) & (lane < WIDE * slot + WIDE), turned, edge)
            right = jnp.where(inner_left, pltpu.roll(edge, 127, 1), pltpu.roll(v, 127, 1))
            left = jnp.where(inner_right, pltpu.roll(edge, 1, 1), pltpu.roll(v, 1, 1))
            other = strips[f, 1 - parity, pl.ds(low, 8), :]
            across = pltpu.roll(other, WIDE if parity == 0 else 128 - WIDE, 1)
            total = grow_sides(strips, (f, parity), low, v, top, bottom)
            total = total + (other + across) + (right + left)
            center.append(v)
            laplace.append(total - 6.0 * v)
        return cell_step(center, laplace)

    state = (main_a, strip_a, main_b, strip_b)
    for step in range(1, STEPS + 1):
        src, strips, dst, strips_dst = state
        early = step <= STEPS_BEFORE
        top = plan.own - 1 if early else plan.first + plan.planes - 1
        bottom = None if early else plan.first
        if step < STEPS:
            def row_step(row, carry):
                for tile in range(plan.tiles):
                    low = plan.start + 8 * tile
                    new = main_tile(src, strips, row, low, top, bottom)
                    for f in range(6):
                        dst[f, row, pl.ds(low, 8), :] = new[f]
                return carry

            lax.fori_loop(step, tall - step, row_step, 0)
            for tile in range(plan.tiles):
                for parity in range(2):
                    low = plan.start + 8 * tile
                    new = strip_tile(src, strips, parity, low, top, bottom)
                    for f in range(6):
                        strips_dst[f, parity, pl.ds(low, 8), :] = new[f]
        else:
            def row_last(row, carry):
                for tile in range(plan.planes // 8):
                    low = plan.first + 8 * tile
                    new = main_tile(src, strips, row + STEPS, low, top, bottom)
                    at = pl.ds(8 * tile * rows + row, 8, stride=rows)
                    for f in range(4):
                        phases[f, at, :] = new[f]
                    for i in range(2):
                        potentials[i, at, :] = new[4 + i]
                return carry

            lax.fori_loop(0, rows, row_last, 0)
        if step == STEPS_BEFORE:
            melt = (slice(plan.own, plan.own + plan.shift), slice(None))

            @pl.when(is_last)
            def _():
                def fill(row, carry):
                    unpack(main0, dst, (row,) + melt)
                    return carry

                lax.fori_loop(0, tall, fill, 0)
                for parity in range(2):
                    unpack(strip0, strips_dst, (parity,) + melt)

        state = (dst, strips_dst, src, strips)


def on_device(mesh_shape, labels, potential, melt_codes, melt_table):
    planes, rows, width = labels.shape
    shift, levels = melt_codes.shape[0], melt_table.shape[1]
    plan = Plan(planes, rows, shift)
    flat = planes * rows
    vmem = pl.BlockSpec(memory_space=pltpu.VMEM)
    smem = pl.BlockSpec(memory_space=pltpu.SMEM)
    f32 = jnp.float32
    dma = pltpu.SemaphoreType.DMA
    main0, strip0 = pl.pallas_call(
        functools.partial(gather_kernel, plan, mesh_shape, levels),
        out_shape=(
            jax.ShapeDtypeStruct((3, plan.tall, plan.deep, width), f32),
            jax.ShapeDtypeStruct((3, 2, plan.deep, width), f32),
        ),
        in_specs=[vmem, vmem, vmem, smem],
        out_specs=(vmem, vmem),
        scratch_shapes=[
            pltpu.VMEM((plan.above * rows, width), jnp.int32),
            pltpu.VMEM((2, plan.above * rows, width), f32),
            pltpu.VMEM((3, 2, plan.deep, width), f32),
            dma((3,)), dma((3,)), dma((12,)), dma((12,)), dma((3,)), dma((3,)),
        ],
        compiler_params=pltpu.CompilerParams(collective_id=0, has_side_effects=True),
        name="gather",
    )(labels.reshape(flat, width), potential.reshape(2, flat, width), melt_codes.reshape(shift * rows, width), melt_table)
    phases, potentials = pl.pallas_call(
        functools.partial(steps_kernel, plan, mesh_shape[0]),
        out_shape=(
            jax.ShapeDtypeStruct((4, flat, width), f32),
            jax.ShapeDtypeStruct((2, flat, width), f32),
        ),
        in_specs=[vmem, vmem],
        out_specs=(vmem, vmem),
        scratch_shapes=[
            pltpu.VMEM((6, plan.tall, plan.deep, width), f32),
            pltpu.VMEM((6, plan.tall, plan.deep, width), f32),
            pltpu.VMEM((6, 2, plan.deep, width), f32),
            pltpu.VMEM((6, 2, plan.deep, width), f32),
        ],
        name="steps",
    )(main0, strip0)
    return phases.reshape(4, planes, rows, width), potentials.reshape(2, planes, rows, width)


def solution(mesh):
    mesh_shape = tuple(mesh.shape[axis] for axis in ("grow", "gy", "gz"))
    return jax.shard_map(
        functools.partial(on_device, mesh_shape),
        mesh=mesh,
        in_specs=(P("grow", "gy", "gz"), P(None, "grow", "gy", "gz"), P(None, "gy", "gz"), P()),
        out_specs=(P(None, "grow", "gy", "gz"), P(None, "grow", "gy", "gz")),
        check_vma=False,
    )
```

```python
import functools

import jax
import jax.numpy as jnp
from jax import lax
from jax.experimental import pallas as pl
from jax.experimental.pallas import tpu as pltpu
from jax.sharding import PartitionSpec as P

STEPS_BEFORE = 3
STEPS_AFTER = 2
STEPS = STEPS_BEFORE + STEPS_AFTER
HALF = 7
WIDE = 2 * HALF
MESH = pl.DeviceIdType.MESH


class Plan:
    def __init__(self, planes, rows, shift):
        self.planes, self.rows, self.shift = planes, rows, shift
        self.skip = (shift - STEPS) // 8 * 8
        self.own = planes - self.skip
        self.above = shift + STEPS
        self.upper = -(-self.above // 8) * 8
        self.deep = self.own + self.upper
        self.first = shift - self.skip
        self.start = self.first - STEPS + 1
        self.tiles = -(-(planes + 2 * (STEPS - 1)) // 8)
        self.tall = rows + 2 * STEPS
        self.slots = self.tall // 2


def gather_kernel(plan, mesh_shape, levels, lab, pot, codes, table, main, strip, pack, lab_up, pot_up, g_send, g_recv, y_send, y_recv, z_send, z_recv):
    g, y, z = lax.axis_index("grow"), lax.axis_index("gy"), lax.axis_index("gz")
    count_g, count_y, count_z = mesh_shape
    rows, own, tall = plan.rows, plan.own, plan.tall
    has_below, has_above = g > 0, g < count_g - 1
    y_up, y_down = lax.rem(y + 1, count_y), lax.rem(y + count_y - 1, count_y)
    z_other = lax.rem(z + 1, count_z)

    barrier = pltpu.get_barrier_semaphore()

    def greet(target):
        pl.semaphore_signal(barrier, inc=1, device_id=target, device_id_type=MESH)

    @pl.when(has_below)
    def _():
        greet((g - 1, y, z))

    @pl.when(has_above)
    def _():
        greet((g + 1, y, z))

    greet((g, y_up, z))
    greet((g, y_down, z))
    greet((g, y, z_other))
    pl.semaphore_wait(barrier, 3 + has_below.astype(jnp.int32) + has_above.astype(jnp.int32))

    def g_copy(i):
        size = plan.above * rows
        src = lab.at[pl.ds(0, size)] if i == 0 else pot.at[i - 1, pl.ds(0, size)]
        dst = lab_up if i == 0 else pot_up.at[i - 1]
        return pltpu.make_async_remote_copy(
            src_ref=src, dst_ref=dst, send_sem=g_send.at[i], recv_sem=g_recv.at[i],
            device_id=(g - 1, y, z), device_id_type=MESH)

    @pl.when(has_below)
    def _():
        for i in range(3):
            g_copy(i).start()

    def y_copy(slot, values, low, size, up):
        if up:
            src, dst, target = rows, 0, y_up
        else:
            src, dst, target = STEPS, STEPS + rows, y_down
        return pltpu.make_async_remote_copy(
            src_ref=main.at[values, pl.ds(src, STEPS), pl.ds(low, size)],
            dst_ref=main.at[values, pl.ds(dst, STEPS), pl.ds(low, size)],
            send_sem=y_send.at[slot], recv_sem=y_recv.at[slot],
            device_id=(g, target, z), device_id_type=MESH)

    def row_of(ref, i, row, begin, size):
        at = pl.ds(begin * rows + row, size, stride=rows)
        return ref[at].astype(jnp.float32) if i == 0 else ref[i - 1, at]

    own_copies = []
    for i in range(3):
        for row in range(rows):
            main[i, STEPS + row, 0:own] = row_of(lab if i == 0 else pot, i, row, plan.skip, own)
        for up in (True, False):
            copy = y_copy(2 * i + up, i, 0, own, up)
            copy.start()
            own_copies.append(copy)

    up_copies = []
    for i in range(3):
        @pl.when(has_above)
        def _(i=i):
            g_copy(i).wait_recv()
            for row in range(rows):
                main[i, STEPS + row, own : own + plan.above] = row_of(lab_up if i == 0 else pot_up, i, row, 0, plan.above)
                rest = plan.upper - plan.above
                if rest:
                    main[i, STEPS + row, own + plan.above : plan.deep] = jnp.zeros((rest, 128), jnp.float32)

        @pl.when(jnp.logical_not(has_above))
        def _(i=i):
            for row in range(rows):
                if i == 0:
                    main[0, STEPS + row, own : own + plan.shift] = jnp.full((plan.shift, 128), 3.0, jnp.float32)
                else:
                    code = codes[pl.ds(row, plan.shift, stride=rows)]
                    value = jnp.zeros((plan.shift, 128), jnp.float32)
                    for level in range(levels):
                        value = jnp.where(code == level, table[i - 1, level], value)
                    main[i, STEPS + row, own : own + plan.shift] = value
                left = plan.deep - own - plan.shift
                main[i, STEPS + row, own + plan.shift : plan.deep] = jnp.zeros((left, 128), jnp.float32)

        for up in (True, False):
            copy = y_copy(6 + 2 * i + up, i, own, plan.upper, up)
            copy.start()
            up_copies.append(copy)

    lane = lax.broadcasted_iota(jnp.int32, (plan.deep, 128), 1)
    z_copies = []
    for i in range(3):
        for copy in own_copies[2 * i : 2 * i + 2] + up_copies[2 * i : 2 * i + 2]:
            copy.wait_recv()
        for parity in range(2):
            packed = jnp.zeros((plan.deep, 128), jnp.float32)
            for slot in range(plan.slots):
                turned = pltpu.roll(main[i, 2 * slot + parity], WIDE * slot + HALF, 1)
                inside = (lane >= WIDE * slot) & (lane < WIDE * slot + WIDE)
                packed = jnp.where(inside, turned, packed)
            pack[i, parity] = packed
        copy = pltpu.make_async_remote_copy(
            src_ref=pack.at[i], dst_ref=strip.at[i], send_sem=z_send.at[i], recv_sem=z_recv.at[i],
            device_id=(g, y, z_other), device_id_type=MESH)
        copy.start()
        z_copies.append(copy)

    for copy in z_copies:
        copy.wait()
    for copy in own_copies + up_copies:
        copy.wait_send()

    @pl.when(has_below)
    def _():
        for i in range(3):
            g_copy(i).wait_send()


def cell_step(center, sums):
    p, (m0, m1) = center[:4], center[4:]
    around = sums[:3] + [6.0 - (sums[0] + sums[1] + sums[2])]
    third = 0.3 * (m0 + m1) + 0.15
    minus_w = (third + 2.1 * m0, third + 2.1 * m1, third, 3.5 * third - 0.525)
    squares = [v * v for v in p]
    shared = 0.28 - 0.6 * ((squares[0] + squares[1]) + (squares[2] + squares[3]))
    local = [p[a] * ((shared + minus_w[a]) + p[a] * (0.6 * p[a] - minus_w[a])) for a in range(4)]
    mean = 0.25 * ((local[0] + local[1]) + (local[2] + local[3])) - 0.07
    held = [jnp.clip((0.12 * around[a] - mean) + local[a], 0.0, 1.0) for a in range(4)]
    inverse = 1.0 / ((held[0] + held[1]) + (held[2] + held[3]))
    new = [v * inverse for v in held]
    change = [new[a] * new[a] * (1.5 - new[a]) - squares[a] * (1.5 - p[a]) for a in range(4)]
    release = 0.2 * (change[0] + change[1] + change[2]) + 0.7 * change[3]
    mobility = 0.0075 + 0.1425 * p[3]
    new0 = (m0 + mobility * (sums[3] - 6.0 * m0)) - (release + 1.4 * change[0])
    new1 = (m1 + mobility * (sums[4] - 6.0 * m1)) - (release + 1.4 * change[1])
    return new + [new0, new1]


def steps_kernel(plan, count_g, main0, strip0, edge0, phases, potentials, main_a, main_b, strip_a, strip_b, edges):
    g = lax.axis_index("grow")
    is_first, is_last = g == 0, g == count_g - 1
    rows, tall, deep = plan.rows, plan.tall, plan.deep

    def unpack(source, target, index):
        label = source[(0,) + index]
        for a in range(4):
            target[(a,) + index] = jnp.where(label == float(a), 1.0, 0.0)
        for i in range(2):
            target[(4 + i,) + index] = source[(1 + i,) + index]

    def unpack_row(row, carry):
        unpack(main0, main_a, (row,))
        return carry

    lax.fori_loop(0, tall, unpack_row, 0)
    for parity in range(2):
        unpack(strip0, strip_a, (parity,))
        unpack(edge0, edges, (parity,))

    lane = lax.broadcasted_iota(jnp.int32, (8, 128), 1)
    place = lax.broadcasted_iota(jnp.int32, (8, 128), 0)
    at_left, at_right = lane == 0, lane == 127
    inner_left, inner_right = lane % WIDE == HALF - 1, lane % WIDE == HALF

    def grow_sides(ref, index, low, center, top, bottom):
        above = ref[index + (pl.ds(low + 1, 8), slice(None))]
        below = ref[index + (pl.ds(low - 1, 8), slice(None))]
        if top is not None and low <= top < low + 8:
            above = jnp.where((place == top - low) & is_last, center, above)
        if bottom is not None and low <= bottom < low + 8:
            below = jnp.where((place == bottom - low) & is_first, center, below)
        return above + below

    moving = (0, 1, 2, 4, 5)

    def main_tile(src, strips, row, low, top, bottom):
        slot, parity = row // 2, lax.rem(row, 2)
        turn = 128 - (WIDE * slot + HALF)
        center = [src[f, row, pl.ds(low, 8), :] for f in range(6)]
        sums = []
        for f in moving:
            v = center[f]
            near = pltpu.roll(strips[f, parity, pl.ds(low, 8), :], turn, 1)
            right = pltpu.roll(jnp.where(at_left, near, v), 127, 1)
            left = pltpu.roll(jnp.where(at_right, near, v), 1, 1)
            total = grow_sides(src, (f, row), low, v, top, bottom)
            total = total + (src[f, row + 1, pl.ds(low, 8), :] + src[f, row - 1, pl.ds(low, 8), :])
            sums.append(total + (right + left))
        return cell_step(center, sums)

    def strip_tile(strips, parity, low, top, bottom):
        center = [strips[f, parity, pl.ds(low, 8), :] for f in range(6)]
        sums = []
        for f in moving:
            v = center[f]
            edge = edges[f, parity, pl.ds(low, 8), :]
            right = pltpu.roll(jnp.where(inner_right, edge, v), 127, 1)
            left = pltpu.roll(jnp.where(inner_left, edge, v), 1, 1)
            other = strips[f, 1 - parity, pl.ds(low, 8), :]
            across = pltpu.roll(other, WIDE if parity == 0 else 128 - WIDE, 1)
            total = grow_sides(strips, (f, parity), low, v, top, bottom)
            sums.append(total + (other + across) + (right + left))
        return cell_step(center, sums)

    state = (main_a, strip_a, main_b, strip_b)
    for step in range(1, STEPS + 1):
        src, strips, dst, strips_dst = state
        early = step <= STEPS_BEFORE
        top = plan.own - 1 if early else plan.first + plan.planes - 1
        bottom = None if early else plan.first
        if step < STEPS:
            for tile in range(plan.tiles):
                for parity in range(2):
                    low = plan.start + 8 * tile
                    new = strip_tile(strips, parity, low, top, bottom)
                    for f in range(6):
                        strips_dst[f, parity, pl.ds(low, 8), :] = new[f]

            def row_step(row, carry):
                slot, parity = row // 2, lax.rem(row, 2)
                turn = WIDE * slot + HALF
                inside = (lane == turn) | (lane == turn - 1)
                for tile in range(plan.tiles):
                    low = plan.start + 8 * tile
                    new = main_tile(src, strips, row, low, top, bottom)
                    for f in range(6):
                        dst[f, row, pl.ds(low, 8), :] = new[f]
                        if f in moving and step < STEPS - 1:
                            at = (f, parity, pl.ds(low, 8), slice(None))
                            edges[at] = jnp.where(inside, pltpu.roll(new[f], turn, 1), edges[at])
                return carry

            lax.fori_loop(step, tall - step, row_step, 0)
        else:
            def row_last(row, carry):
                for tile in range(plan.planes // 8):
                    low = plan.first + 8 * tile
                    new = main_tile(src, strips, row + STEPS, low, top, bottom)
                    at = pl.ds(8 * tile * rows + row, 8, stride=rows)
                    for f in range(4):
                        phases[f, at, :] = new[f]
                    for i in range(2):
                        potentials[i, at, :] = new[4 + i]
                return carry

            lax.fori_loop(0, rows, row_last, 0)
        if step == STEPS_BEFORE:
            melt = (slice(plan.own, plan.own + plan.shift), slice(None))

            @pl.when(is_last)
            def _():
                def fill(row, carry):
                    unpack(main0, dst, (row,) + melt)
                    return carry

                lax.fori_loop(0, tall, fill, 0)
                for parity in range(2):
                    unpack(strip0, strips_dst, (parity,) + melt)
                    unpack(edge0, edges, (parity,) + melt)

        state = (dst, strips_dst, src, strips)


def on_device(mesh_shape, labels, potential, melt_codes, melt_table):
    planes, rows, width = labels.shape
    shift, levels = melt_codes.shape[0], melt_table.shape[1]
    plan = Plan(planes, rows, shift)
    flat = planes * rows
    vmem = pl.BlockSpec(memory_space=pltpu.VMEM)
    smem = pl.BlockSpec(memory_space=pltpu.SMEM)
    f32 = jnp.float32
    dma = pltpu.SemaphoreType.DMA
    main0, strip0, edge0 = pl.pallas_call(
        functools.partial(gather_kernel, plan, mesh_shape, levels),
        out_shape=(
            jax.ShapeDtypeStruct((3, plan.tall, plan.deep, width), f32),
            jax.ShapeDtypeStruct((3, 2, plan.deep, width), f32),
            jax.ShapeDtypeStruct((3, 2, plan.deep, width), f32),
        ),
        in_specs=[vmem, vmem, vmem, smem],
        out_specs=(vmem, vmem, vmem),
        scratch_shapes=[
            pltpu.VMEM((plan.above * rows, width), jnp.int32),
            pltpu.VMEM((2, plan.above * rows, width), f32),
            dma((3,)), dma((3,)), dma((12,)), dma((12,)), dma((3,)), dma((3,)),
        ],
        compiler_params=pltpu.CompilerParams(collective_id=0, has_side_effects=True),
        name="gather",
    )(labels.reshape(flat, width), potential.reshape(2, flat, width), melt_codes.reshape(shift * rows, width), melt_table)
    phases, potentials = pl.pallas_call(
        functools.partial(steps_kernel, plan, mesh_shape[0]),
        out_shape=(
            jax.ShapeDtypeStruct((4, flat, width), f32),
            jax.ShapeDtypeStruct((2, flat, width), f32),
        ),
        in_specs=[vmem, vmem, vmem],
        out_specs=(vmem, vmem),
        scratch_shapes=[
            pltpu.VMEM((6, plan.tall, plan.deep, width), f32),
            pltpu.VMEM((6, plan.tall, plan.deep, width), f32),
            pltpu.VMEM((6, 2, plan.deep, width), f32),
            pltpu.VMEM((6, 2, plan.deep, width), f32),
            pltpu.VMEM((6, 2, plan.deep, width), f32),
        ],
        name="steps",
    )(main0, strip0, edge0)
    return phases.reshape(4, planes, rows, width), potentials.reshape(2, planes, rows, width)


def solution(mesh):
    mesh_shape = tuple(mesh.shape[axis] for axis in ("grow", "gy", "gz"))
    return jax.shard_map(
        functools.partial(on_device, mesh_shape),
        mesh=mesh,
        in_specs=(P("grow", "gy", "gz"), P(None, "grow", "gy", "gz"), P(None, "gy", "gz"), P()),
        out_specs=(P(None, "grow", "gy", "gz"), P(None, "grow", "gy", "gz")),
        check_vma=False,
    )
```

```python
import functools

import jax
import jax.numpy as jnp
from jax import lax
from jax.experimental import pallas as pl
from jax.experimental.pallas import tpu as pltpu
from jax.sharding import PartitionSpec as P

STEPS_BEFORE = 3
STEPS_AFTER = 2
STEPS = STEPS_BEFORE + STEPS_AFTER
HALF = 7
WIDE = 2 * HALF
MESH = pl.DeviceIdType.MESH


class Plan:
    def __init__(self, planes, rows, shift):
        self.planes, self.rows, self.shift = planes, rows, shift
        self.skip = (shift - STEPS) // 8 * 8
        self.own = planes - self.skip
        self.above = shift + STEPS
        self.upper = -(-self.above // 8) * 8
        self.deep = self.own + self.upper
        self.first = shift - self.skip
        self.start = self.first - STEPS + 1
        self.tiles = -(-(planes + 2 * (STEPS - 1)) // 8)
        self.tall = rows + 2 * STEPS
        self.slots = self.tall // 2


def gather_kernel(plan, mesh_shape, levels, lab, pot, codes, table, main, strip, pack, lab_up, pot_up, g_send, g_recv, y_send, y_recv, z_send, z_recv):
    g, y, z = lax.axis_index("grow"), lax.axis_index("gy"), lax.axis_index("gz")
    count_g, count_y, count_z = mesh_shape
    rows, own, tall = plan.rows, plan.own, plan.tall
    has_below, has_above = g > 0, g < count_g - 1
    y_up, y_down = lax.rem(y + 1, count_y), lax.rem(y + count_y - 1, count_y)
    z_other = lax.rem(z + 1, count_z)

    barrier = pltpu.get_barrier_semaphore()

    def greet(target):
        pl.semaphore_signal(barrier, inc=1, device_id=target, device_id_type=MESH)

    @pl.when(has_below)
    def _():
        greet((g - 1, y, z))

    @pl.when(has_above)
    def _():
        greet((g + 1, y, z))

    greet((g, y_up, z))
    greet((g, y_down, z))
    greet((g, y, z_other))
    pl.semaphore_wait(barrier, 3 + has_below.astype(jnp.int32) + has_above.astype(jnp.int32))

    split = (0, plan.upper // 3 // 8 * 8, plan.upper)
    pieces = [(piece, i) for i in range(3) for piece in range(2)]

    def g_copy(piece, i):
        begin, end = split[piece], min(split[piece + 1], plan.above)
        at = pl.ds(begin * rows, (end - begin) * rows)
        src, dst = (lab.at[at], lab_up.at[at]) if i == 0 else (pot.at[i - 1, at], pot_up.at[i - 1, at])
        sem = 3 * piece + i
        return pltpu.make_async_remote_copy(
            src_ref=src, dst_ref=dst, send_sem=g_send.at[sem], recv_sem=g_recv.at[sem],
            device_id=(g - 1, y, z), device_id_type=MESH)

    @pl.when(has_below)
    def _():
        for piece, i in pieces:
            g_copy(piece, i).start()

    def y_copies(part, i, low, size):
        copies = []
        for up in range(2):
            src, dst, target = (rows, 0, y_up) if up else (STEPS, STEPS + rows, y_down)
            sem = 2 * (3 * part + i) + up
            copy = pltpu.make_async_remote_copy(
                src_ref=main.at[i, pl.ds(src, STEPS), pl.ds(low, size)],
                dst_ref=main.at[i, pl.ds(dst, STEPS), pl.ds(low, size)],
                send_sem=y_send.at[sem], recv_sem=y_recv.at[sem],
                device_id=(g, target, z), device_id_type=MESH)
            copy.start()
            copies.append(copy)
        return copies

    def row_of(ref, i, row, begin, size):
        at = pl.ds(begin * rows + row, size, stride=rows)
        return ref[at].astype(jnp.float32) if i == 0 else ref[i - 1, at]

    y_sent = {}
    for i in range(3):
        for row in range(rows):
            main[i, STEPS + row, 0:own] = row_of(lab if i == 0 else pot, i, row, plan.skip, own)
        y_sent[0, i] = y_copies(0, i, 0, own)

    def z_copy(part, i, low, size):
        for copy in y_sent[part, i]:
            copy.wait_recv()
        lane = lax.broadcasted_iota(jnp.int32, (size, 128), 1)
        for parity in range(2):
            packed = jnp.zeros((size, 128), jnp.float32)
            for slot in range(plan.slots):
                turned = pltpu.roll(main[i, 2 * slot + parity, low : low + size], WIDE * slot + HALF, 1)
                packed = jnp.where((lane >= WIDE * slot) & (lane < WIDE * slot + WIDE), turned, packed)
            pack[i, parity, low : low + size] = packed
        sem = 3 * part + i
        at = (i, slice(None), pl.ds(low, size))
        copy = pltpu.make_async_remote_copy(
            src_ref=pack.at[at], dst_ref=strip.at[at], send_sem=z_send.at[sem], recv_sem=z_recv.at[sem],
            device_id=(g, y, z_other), device_id_type=MESH)
        copy.start()
        return copy

    def enter(piece, i):
        begin, end = split[piece], split[piece + 1]
        filled = min(end, plan.above)

        @pl.when(has_above)
        def _():
            g_copy(piece, i).wait_recv()
            for row in range(rows):
                main[i, STEPS + row, own + begin : own + filled] = row_of(lab_up if i == 0 else pot_up, i, row, begin, filled - begin)
                if end > filled:
                    main[i, STEPS + row, own + filled : own + end] = jnp.zeros((end - filled, 128), jnp.float32)

        @pl.when(jnp.logical_not(has_above))
        def _():
            melt_end = min(end, plan.shift)
            for row in range(rows):
                if i == 0:
                    value = jnp.full((melt_end - begin, 128), 3.0, jnp.float32)
                else:
                    code = codes[pl.ds(begin * rows + row, melt_end - begin, stride=rows)]
                    value = jnp.zeros((melt_end - begin, 128), jnp.float32)
                    for level in range(levels):
                        value = jnp.where(code == level, table[i - 1, level], value)
                main[i, STEPS + row, own + begin : own + melt_end] = value
                if end > melt_end:
                    main[i, STEPS + row, own + melt_end : own + end] = jnp.zeros((end - melt_end, 128), jnp.float32)

        y_sent[1 + piece, i] = y_copies(1 + piece, i, own + begin, end - begin)

    z_sent = []
    for i in range(3):
        enter(0, i)
        enter(1, i)
        z_sent.append(z_copy(0, i, 0, own))
    for piece, i in pieces:
        z_sent.append(z_copy(1 + piece, i, own + split[piece], split[piece + 1] - split[piece]))

    for copy in z_sent:
        copy.wait()
    for copies in y_sent.values():
        for copy in copies:
            copy.wait_send()

    @pl.when(has_below)
    def _():
        for piece, i in pieces:
            g_copy(piece, i).wait_send()


def cell_step(center, sums):
    p, (m0, m1) = center[:4], center[4:]
    around = sums[:3] + [6.0 - (sums[0] + sums[1] + sums[2])]
    third = 0.3 * (m0 + m1) + 0.15
    minus_w = (third + 2.1 * m0, third + 2.1 * m1, third, 3.5 * third - 0.525)
    squares = [v * v for v in p]
    shared = 0.28 - 0.6 * ((squares[0] + squares[1]) + (squares[2] + squares[3]))
    local = [p[a] * ((shared + minus_w[a]) + p[a] * (0.6 * p[a] - minus_w[a])) for a in range(4)]
    mean = 0.25 * ((local[0] + local[1]) + (local[2] + local[3])) - 0.07
    held = [jnp.clip((0.12 * around[a] - mean) + local[a], 0.0, 1.0) for a in range(4)]
    inverse = 1.0 / ((held[0] + held[1]) + (held[2] + held[3]))
    new = [v * inverse for v in held]
    change = [new[a] * new[a] * (1.5 - new[a]) - squares[a] * (1.5 - p[a]) for a in range(4)]
    release = 0.2 * (change[0] + change[1] + change[2]) + 0.7 * change[3]
    mobility = 0.0075 + 0.1425 * p[3]
    new0 = (m0 + mobility * (sums[3] - 6.0 * m0)) - (release + 1.4 * change[0])
    new1 = (m1 + mobility * (sums[4] - 6.0 * m1)) - (release + 1.4 * change[1])
    return new + [new0, new1]


def steps_kernel(plan, count_g, main0, strip0, edge0, phases, potentials, main_a, main_b, strip_a, strip_b, edges):
    g = lax.axis_index("grow")
    is_first, is_last = g == 0, g == count_g - 1
    rows, tall, deep = plan.rows, plan.tall, plan.deep

    def unpack(source, target, index):
        label = source[(0,) + index]
        for a in range(4):
            target[(a,) + index] = jnp.where(label == float(a), 1.0, 0.0)
        for i in range(2):
            target[(4 + i,) + index] = source[(1 + i,) + index]

    def unpack_row(row, carry):
        unpack(main0, main_a, (row,))
        return carry

    lax.fori_loop(0, tall, unpack_row, 0)
    for parity in range(2):
        unpack(strip0, strip_a, (parity,))
        unpack(edge0, edges, (parity,))

    lane = lax.broadcasted_iota(jnp.int32, (8, 128), 1)
    place = lax.broadcasted_iota(jnp.int32, (8, 128), 0)
    at_left, at_right = lane == 0, lane == 127
    inner_left, inner_right = lane % WIDE == HALF - 1, lane % WIDE == HALF

    def grow_sides(ref, index, low, center, top, bottom):
        above = ref[index + (pl.ds(low + 1, 8), slice(None))]
        below = ref[index + (pl.ds(low - 1, 8), slice(None))]
        if top is not None and low <= top < low + 8:
            above = jnp.where((place == top - low) & is_last, center, above)
        if bottom is not None and low <= bottom < low + 8:
            below = jnp.where((place == bottom - low) & is_first, center, below)
        return above + below

    moving = (0, 1, 2, 4, 5)

    def main_tile(src, strips, row, parity, slot, low, top, bottom):
        turn = 128 - (WIDE * slot + HALF)
        center = [src[f, row, pl.ds(low, 8), :] for f in range(6)]
        sums = []
        for f in moving:
            v = center[f]
            near = pltpu.roll(strips[f, parity, pl.ds(low, 8), :], turn, 1)
            right = pltpu.roll(jnp.where(at_left, near, v), 127, 1)
            left = pltpu.roll(jnp.where(at_right, near, v), 1, 1)
            total = grow_sides(src, (f, row), low, v, top, bottom)
            total = total + (src[f, row + 1, pl.ds(low, 8), :] + src[f, row - 1, pl.ds(low, 8), :])
            sums.append(total + (right + left))
        return cell_step(center, sums)

    def strip_tile(strips, parity, low, top, bottom):
        center = [strips[f, parity, pl.ds(low, 8), :] for f in range(6)]
        sums = []
        for f in moving:
            v = center[f]
            edge = edges[f, parity, pl.ds(low, 8), :]
            right = pltpu.roll(jnp.where(inner_right, edge, v), 127, 1)
            left = pltpu.roll(jnp.where(inner_left, edge, v), 1, 1)
            other = strips[f, 1 - parity, pl.ds(low, 8), :]
            across = pltpu.roll(other, WIDE if parity == 0 else 128 - WIDE, 1)
            total = grow_sides(strips, (f, parity), low, v, top, bottom)
            sums.append(total + (other + across) + (right + left))
        return cell_step(center, sums)

    state = (main_a, strip_a, main_b, strip_b)
    for step in range(1, STEPS + 1):
        src, strips, dst, strips_dst = state
        early = step <= STEPS_BEFORE
        top = plan.own - 1 if early else plan.first + plan.planes - 1
        bottom = None if early else plan.first
        if step < STEPS:
            for tile in range(plan.tiles):
                for parity in range(2):
                    low = plan.start + 8 * tile
                    new = strip_tile(strips, parity, low, top, bottom)
                    for f in range(6):
                        strips_dst[f, parity, pl.ds(low, 8), :] = new[f]

            def pair_step(pair, carry):
                for part in range(2):
                    row, parity = 2 * pair + step + part, (step + part) % 2
                    slot = pair + (step + part) // 2
                    turn = WIDE * slot + HALF
                    inside = (lane == turn) | (lane == turn - 1)
                    for tile in range(plan.tiles):
                        low = plan.start + 8 * tile
                        new = main_tile(src, strips, row, parity, slot, low, top, bottom)
                        for f in range(6):
                            dst[f, row, pl.ds(low, 8), :] = new[f]
                            if f in moving and step < STEPS - 1:
                                at = (f, parity, pl.ds(low, 8), slice(None))
                                edges[at] = jnp.where(inside, pltpu.roll(new[f], turn, 1), edges[at])
                return carry

            lax.fori_loop(0, (tall - 2 * step) // 2, pair_step, 0)
        else:
            def pair_last(pair, carry):
                for part in range(2):
                    row, parity = 2 * pair + part, (STEPS + part) % 2
                    slot = pair + (STEPS + part) // 2
                    for tile in range(plan.planes // 8):
                        low = plan.first + 8 * tile
                        new = main_tile(src, strips, row + STEPS, parity, slot, low, top, bottom)
                        at = pl.ds(8 * tile * rows + row, 8, stride=rows)
                        for f in range(4):
                            phases[f, at, :] = new[f]
                        for i in range(2):
                            potentials[i, at, :] = new[4 + i]
                return carry

            lax.fori_loop(0, rows // 2, pair_last, 0)
        if step == STEPS_BEFORE:
            melt = (slice(plan.own, plan.own + plan.shift), slice(None))

            @pl.when(is_last)
            def _():
                def fill(row, carry):
                    unpack(main0, dst, (row,) + melt)
                    return carry

                lax.fori_loop(0, tall, fill, 0)
                for parity in range(2):
                    unpack(strip0, strips_dst, (parity,) + melt)
                    unpack(edge0, edges, (parity,) + melt)

        state = (dst, strips_dst, src, strips)


def on_device(mesh_shape, labels, potential, melt_codes, melt_table):
    planes, rows, width = labels.shape
    shift, levels = melt_codes.shape[0], melt_table.shape[1]
    plan = Plan(planes, rows, shift)
    flat = planes * rows
    vmem = pl.BlockSpec(memory_space=pltpu.VMEM)
    smem = pl.BlockSpec(memory_space=pltpu.SMEM)
    f32 = jnp.float32
    dma = pltpu.SemaphoreType.DMA
    main0, strip0, edge0 = pl.pallas_call(
        functools.partial(gather_kernel, plan, mesh_shape, levels),
        out_shape=(
            jax.ShapeDtypeStruct((3, plan.tall, plan.deep, width), f32),
            jax.ShapeDtypeStruct((3, 2, plan.deep, width), f32),
            jax.ShapeDtypeStruct((3, 2, plan.deep, width), f32),
        ),
        in_specs=[vmem, vmem, vmem, smem],
        out_specs=(vmem, vmem, vmem),
        scratch_shapes=[
            pltpu.VMEM((plan.above * rows, width), jnp.int32),
            pltpu.VMEM((2, plan.above * rows, width), f32),
            dma((6,)), dma((6,)), dma((18,)), dma((18,)), dma((9,)), dma((9,)),
        ],
        compiler_params=pltpu.CompilerParams(collective_id=0, has_side_effects=True),
        name="gather",
    )(labels.reshape(flat, width), potential.reshape(2, flat, width), melt_codes.reshape(shift * rows, width), melt_table)
    phases, potentials = pl.pallas_call(
        functools.partial(steps_kernel, plan, mesh_shape[0]),
        out_shape=(
            jax.ShapeDtypeStruct((4, flat, width), f32),
            jax.ShapeDtypeStruct((2, flat, width), f32),
        ),
        in_specs=[vmem, vmem, vmem],
        out_specs=(vmem, vmem),
        scratch_shapes=[
            pltpu.VMEM((6, plan.tall, plan.deep, width), f32),
            pltpu.VMEM((6, plan.tall, plan.deep, width), f32),
            pltpu.VMEM((6, 2, plan.deep, width), f32),
            pltpu.VMEM((6, 2, plan.deep, width), f32),
            pltpu.VMEM((6, 2, plan.deep, width), f32),
        ],
        name="steps",
    )(main0, strip0, edge0)
    return phases.reshape(4, planes, rows, width), potentials.reshape(2, planes, rows, width)


def solution(mesh):
    mesh_shape = tuple(mesh.shape[axis] for axis in ("grow", "gy", "gz"))
    return jax.shard_map(
        functools.partial(on_device, mesh_shape),
        mesh=mesh,
        in_specs=(P("grow", "gy", "gz"), P(None, "grow", "gy", "gz"), P(None, "gy", "gz"), P()),
        out_specs=(P(None, "grow", "gy", "gz"), P(None, "grow", "gy", "gz")),
        check_vma=False,
    )
```

```python
import functools

import jax
import jax.numpy as jnp
from jax import lax
from jax.experimental import pallas as pl
from jax.experimental.pallas import tpu as pltpu
from jax.sharding import PartitionSpec as P

STEPS_BEFORE = 3
STEPS_AFTER = 2
STEPS = STEPS_BEFORE + STEPS_AFTER
HALF = 7
WIDE = 2 * HALF
MESH = pl.DeviceIdType.MESH


class Plan:
    def __init__(self, planes, rows, shift):
        self.planes, self.rows, self.shift = planes, rows, shift
        self.skip = (shift - STEPS) // 8 * 8
        self.own = planes - self.skip
        self.above = shift + STEPS
        self.upper = -(-self.above // 8) * 8
        self.deep = self.own + self.upper
        self.first = shift - self.skip
        self.start = self.first - STEPS + 1
        self.tiles = -(-(planes + 2 * (STEPS - 1)) // 8)
        self.tall = rows + 2 * STEPS
        self.slots = self.tall // 2


def gather_kernel(plan, mesh_shape, levels, lab, pot, codes, table, main, strip, pack, lab_up, pot_up, g_send, g_recv, y_send, y_recv, z_send, z_recv):
    g, y, z = lax.axis_index("grow"), lax.axis_index("gy"), lax.axis_index("gz")
    count_g, count_y, count_z = mesh_shape
    rows, own, tall = plan.rows, plan.own, plan.tall
    has_below, has_above = g > 0, g < count_g - 1
    y_up, y_down = lax.rem(y + 1, count_y), lax.rem(y + count_y - 1, count_y)
    z_other = lax.rem(z + 1, count_z)

    barrier = pltpu.get_barrier_semaphore()

    def greet(target):
        pl.semaphore_signal(barrier, inc=1, device_id=target, device_id_type=MESH)

    @pl.when(has_below)
    def _():
        greet((g - 1, y, z))

    @pl.when(has_above)
    def _():
        greet((g + 1, y, z))

    greet((g, y_up, z))
    greet((g, y_down, z))
    greet((g, y, z_other))
    pl.semaphore_wait(barrier, 3 + has_below.astype(jnp.int32) + has_above.astype(jnp.int32))

    split = (0, plan.upper // 3 // 8 * 8, plan.upper)
    pieces = [(piece, i) for i in range(3) for piece in range(2)]

    def g_copy(piece, i):
        begin, end = split[piece], min(split[piece + 1], plan.above)
        at = pl.ds(begin * rows, (end - begin) * rows)
        src, dst = (lab.at[at], lab_up.at[at]) if i == 0 else (pot.at[i - 1, at], pot_up.at[i - 1, at])
        sem = 3 * piece + i
        return pltpu.make_async_remote_copy(
            src_ref=src, dst_ref=dst, send_sem=g_send.at[sem], recv_sem=g_recv.at[sem],
            device_id=(g - 1, y, z), device_id_type=MESH)

    @pl.when(has_below)
    def _():
        for piece, i in pieces:
            g_copy(piece, i).start()

    def y_copies(part, i, low, size):
        copies = []
        for up in range(2):
            src, dst, target = (rows, 0, y_up) if up else (STEPS, STEPS + rows, y_down)
            sem = 2 * (3 * part + i) + up
            copy = pltpu.make_async_remote_copy(
                src_ref=main.at[i, pl.ds(src, STEPS), pl.ds(low, size)],
                dst_ref=main.at[i, pl.ds(dst, STEPS), pl.ds(low, size)],
                send_sem=y_send.at[sem], recv_sem=y_recv.at[sem],
                device_id=(g, target, z), device_id_type=MESH)
            copy.start()
            copies.append(copy)
        return copies

    def row_of(ref, i, row, begin, size):
        at = pl.ds(begin * rows + row, size, stride=rows)
        return ref[at].astype(jnp.float32) if i == 0 else ref[i - 1, at]

    y_sent = {}
    for i in range(3):
        for row in range(rows):
            main[i, STEPS + row, 0:own] = row_of(lab if i == 0 else pot, i, row, plan.skip, own)
        y_sent[0, i] = y_copies(0, i, 0, own)

    def z_copy(part, i, low, size):
        for copy in y_sent[part, i]:
            copy.wait_recv()
        lane = lax.broadcasted_iota(jnp.int32, (size, 128), 1)
        for parity in range(2):
            packed = jnp.zeros((size, 128), jnp.float32)
            for slot in range(plan.slots):
                turned = pltpu.roll(main[i, 2 * slot + parity, low : low + size], WIDE * slot + HALF, 1)
                packed = jnp.where((lane >= WIDE * slot) & (lane < WIDE * slot + WIDE), turned, packed)
            pack[i, parity, low : low + size] = packed
        sem = 3 * part + i
        at = (i, slice(None), pl.ds(low, size))
        copy = pltpu.make_async_remote_copy(
            src_ref=pack.at[at], dst_ref=strip.at[at], send_sem=z_send.at[sem], recv_sem=z_recv.at[sem],
            device_id=(g, y, z_other), device_id_type=MESH)
        copy.start()
        return copy

    def enter(piece, i):
        begin, end = split[piece], split[piece + 1]
        filled = min(end, plan.above)

        @pl.when(has_above)
        def _():
            g_copy(piece, i).wait_recv()
            for row in range(rows):
                main[i, STEPS + row, own + begin : own + filled] = row_of(lab_up if i == 0 else pot_up, i, row, begin, filled - begin)
                if end > filled:
                    main[i, STEPS + row, own + filled : own + end] = jnp.zeros((end - filled, 128), jnp.float32)

        @pl.when(jnp.logical_not(has_above))
        def _():
            melt_end = min(end, plan.shift)
            for row in range(rows):
                if i == 0:
                    value = jnp.full((melt_end - begin, 128), 3.0, jnp.float32)
                else:
                    code = codes[pl.ds(begin * rows + row, melt_end - begin, stride=rows)]
                    value = jnp.zeros((melt_end - begin, 128), jnp.float32)
                    for level in range(levels):
                        value = jnp.where(code == level, table[i - 1, level], value)
                main[i, STEPS + row, own + begin : own + melt_end] = value
                if end > melt_end:
                    main[i, STEPS + row, own + melt_end : own + end] = jnp.zeros((end - melt_end, 128), jnp.float32)

        y_sent[1 + piece, i] = y_copies(1 + piece, i, own + begin, end - begin)

    z_sent = []
    for i in range(3):
        enter(0, i)
        enter(1, i)
        z_sent.append(z_copy(0, i, 0, own))
    for piece, i in pieces:
        z_sent.append(z_copy(1 + piece, i, own + split[piece], split[piece + 1] - split[piece]))

    for copy in z_sent:
        copy.wait()
    for copies in y_sent.values():
        for copy in copies:
            copy.wait_send()

    @pl.when(has_below)
    def _():
        for piece, i in pieces:
            g_copy(piece, i).wait_send()


def cell_step(center, sums):
    p, (m0, m1) = center[:4], center[4:]
    around = sums[:3] + [6.0 - (sums[0] + sums[1] + sums[2])]
    third = 0.3 * (m0 + m1) + 0.15
    minus_w = (third + 2.1 * m0, third + 2.1 * m1, third, 3.5 * third - 0.525)
    squares = [v * v for v in p]
    shared = 0.28 - 0.6 * ((squares[0] + squares[1]) + (squares[2] + squares[3]))
    local = [p[a] * ((shared + minus_w[a]) + p[a] * (0.6 * p[a] - minus_w[a])) for a in range(4)]
    mean = 0.25 * ((local[0] + local[1]) + (local[2] + local[3])) - 0.07
    held = [jnp.clip((0.12 * around[a] - mean) + local[a], 0.0, 1.0) for a in range(4)]
    inverse = 1.0 / ((held[0] + held[1]) + (held[2] + held[3]))
    new = [v * inverse for v in held]
    change = [new[a] * new[a] * (1.5 - new[a]) - squares[a] * (1.5 - p[a]) for a in range(4)]
    release = 0.2 * (change[0] + change[1] + change[2]) + 0.7 * change[3]
    mobility = 0.0075 + 0.1425 * p[3]
    new0 = (m0 + mobility * (sums[3] - 6.0 * m0)) - (release + 1.4 * change[0])
    new1 = (m1 + mobility * (sums[4] - 6.0 * m1)) - (release + 1.4 * change[1])
    return new + [new0, new1]


def steps_kernel(plan, count_g, main0, strip0, edge0, phases, potentials, main_a, main_b, strip_a, strip_b, edges):
    g = lax.axis_index("grow")
    is_first, is_last = g == 0, g == count_g - 1
    rows, tall, deep = plan.rows, plan.tall, plan.deep

    def unpack(source, target, index):
        label = source[(0,) + index]
        for a in range(4):
            target[(a,) + index] = jnp.where(label == float(a), 1.0, 0.0)
        for i in range(2):
            target[(4 + i,) + index] = source[(1 + i,) + index]

    def unpack_row(row, carry):
        unpack(main0, main_a, (row,))
        return carry

    lax.fori_loop(0, tall, unpack_row, 0)
    for parity in range(2):
        unpack(strip0, strip_a, (parity,))
        unpack(edge0, edges, (parity,))

    lane = lax.broadcasted_iota(jnp.int32, (8, 128), 1)
    place = lax.broadcasted_iota(jnp.int32, (8, 128), 0)
    at_left, at_right = lane == 0, lane == 127
    inner_left, inner_right = lane % WIDE == HALF - 1, lane % WIDE == HALF

    def grow_sides(ref, index, low, center, top, bottom):
        above = ref[index + (pl.ds(low + 1, 8), slice(None))]
        below = ref[index + (pl.ds(low - 1, 8), slice(None))]
        if top is not None and low <= top < low + 8:
            above = jnp.where((place == top - low) & is_last, center, above)
        if bottom is not None and low <= bottom < low + 8:
            below = jnp.where((place == bottom - low) & is_first, center, below)
        return above + below

    moving = (0, 1, 2, 4, 5)

    def main_tile(src, strips, row, parity, slot, low, top, bottom):
        turn = 128 - (WIDE * slot + HALF)
        center = [src[f, row, pl.ds(low, 8), :] for f in range(6)]
        sums = []
        for f in moving:
            v = center[f]
            near = pltpu.roll(strips[f, parity, pl.ds(low, 8), :], turn, 1)
            right = pltpu.roll(jnp.where(at_left, near, v), 127, 1)
            left = pltpu.roll(jnp.where(at_right, near, v), 1, 1)
            total = grow_sides(src, (f, row), low, v, top, bottom)
            total = total + (src[f, row + 1, pl.ds(low, 8), :] + src[f, row - 1, pl.ds(low, 8), :])
            sums.append(total + (right + left))
        return cell_step(center, sums)

    def strip_tile(strips, parity, low, top, bottom):
        center = [strips[f, parity, pl.ds(low, 8), :] for f in range(6)]
        sums = []
        for f in moving:
            v = center[f]
            edge = edges[f, parity, pl.ds(low, 8), :]
            right = pltpu.roll(jnp.where(inner_right, edge, v), 127, 1)
            left = pltpu.roll(jnp.where(inner_left, edge, v), 1, 1)
            other = strips[f, 1 - parity, pl.ds(low, 8), :]
            across = pltpu.roll(other, WIDE if parity == 0 else 128 - WIDE, 1)
            total = grow_sides(strips, (f, parity), low, v, top, bottom)
            sums.append(total + (other + across) + (right + left))
        return cell_step(center, sums)

    state = (main_a, strip_a, main_b, strip_b)
    for step in range(1, STEPS + 1):
        src, strips, dst, strips_dst = state
        early = step <= STEPS_BEFORE
        top = plan.own - 1 if early else plan.first + plan.planes - 1
        bottom = None if early else plan.first
        if step < STEPS:
            for tile in range(plan.tiles):
                for parity in range(2):
                    low = plan.start + 8 * tile
                    new = strip_tile(strips, parity, low, top, bottom)
                    for f in range(6):
                        strips_dst[f, parity, pl.ds(low, 8), :] = new[f]

            def pair_step(pair, carry):
                for part in range(2):
                    row, parity = 2 * pair + step + part, (step + part) % 2
                    slot = pair + (step + part) // 2
                    turn = WIDE * slot + HALF
                    inside = (lane == turn) | (lane == turn - 1)
                    for tile in range(plan.tiles):
                        low = plan.start + 8 * tile
                        new = main_tile(src, strips, row, parity, slot, low, top, bottom)
                        for f in range(6):
                            dst[f, row, pl.ds(low, 8), :] = new[f]
                            if f in moving and step < STEPS - 1:
                                at = (f, parity, pl.ds(low, 8), slice(None))
                                edges[at] = jnp.where(inside, pltpu.roll(new[f], turn, 1), edges[at])
                return carry

            lax.fori_loop(0, (tall - 2 * step) // 2, pair_step, 0)
        else:
            def pair_last(pair, carry):
                for part in range(2):
                    row, parity = 2 * pair + part, (STEPS + part) % 2
                    slot = pair + (STEPS + part) // 2
                    for tile in range(plan.planes // 8):
                        low = plan.first + 8 * tile
                        new = main_tile(src, strips, row + STEPS, parity, slot, low, top, bottom)
                        at = pl.ds(8 * tile * rows + row, 8, stride=rows)
                        for f in range(4):
                            phases[f, at, :] = new[f]
                        for i in range(2):
                            potentials[i, at, :] = new[4 + i]
                return carry

            lax.fori_loop(0, rows // 2, pair_last, 0)
        if step == STEPS_BEFORE:
            melt = (slice(plan.own, plan.own + plan.shift), slice(None))

            @pl.when(is_last)
            def _():
                def fill(row, carry):
                    unpack(main0, dst, (row,) + melt)
                    return carry

                lax.fori_loop(0, tall, fill, 0)
                for parity in range(2):
                    unpack(strip0, strips_dst, (parity,) + melt)
                    unpack(edge0, edges, (parity,) + melt)

        state = (dst, strips_dst, src, strips)


def on_device(mesh_shape, labels, potential, melt_codes, melt_table):
    planes, rows, width = labels.shape
    shift, levels = melt_codes.shape[0], melt_table.shape[1]
    plan = Plan(planes, rows, shift)
    flat = planes * rows
    vmem = pl.BlockSpec(memory_space=pltpu.VMEM)
    smem = pl.BlockSpec(memory_space=pltpu.SMEM)
    f32 = jnp.float32
    dma = pltpu.SemaphoreType.DMA
    main0, strip0, edge0 = pl.pallas_call(
        functools.partial(gather_kernel, plan, mesh_shape, levels),
        out_shape=(
            pltpu.VMEM((3, plan.tall, plan.deep, width), f32),
            pltpu.VMEM((3, 2, plan.deep, width), f32),
            pltpu.VMEM((3, 2, plan.deep, width), f32),
        ),
        in_specs=[vmem, vmem, vmem, smem],
        out_specs=(vmem, vmem, vmem),
        scratch_shapes=[
            pltpu.VMEM((plan.above * rows, width), jnp.int32),
            pltpu.VMEM((2, plan.above * rows, width), f32),
            dma((6,)), dma((6,)), dma((18,)), dma((18,)), dma((9,)), dma((9,)),
        ],
        compiler_params=pltpu.CompilerParams(collective_id=0, has_side_effects=True),
        name="gather",
    )(labels.reshape(flat, width), potential.reshape(2, flat, width), melt_codes.reshape(shift * rows, width), melt_table)
    main0, strip0, edge0 = (pltpu.with_memory_space_constraint(v, pltpu.VMEM) for v in (main0, strip0, edge0))
    phases, potentials = pl.pallas_call(
        functools.partial(steps_kernel, plan, mesh_shape[0]),
        out_shape=(
            jax.ShapeDtypeStruct((4, flat, width), f32),
            jax.ShapeDtypeStruct((2, flat, width), f32),
        ),
        in_specs=[vmem, vmem, vmem],
        out_specs=(vmem, vmem),
        scratch_shapes=[
            pltpu.VMEM((6, plan.tall, plan.deep, width), f32),
            pltpu.VMEM((6, plan.tall, plan.deep, width), f32),
            pltpu.VMEM((6, 2, plan.deep, width), f32),
            pltpu.VMEM((6, 2, plan.deep, width), f32),
            pltpu.VMEM((6, 2, plan.deep, width), f32),
        ],
        name="steps",
    )(main0, strip0, edge0)
    return phases.reshape(4, planes, rows, width), potentials.reshape(2, planes, rows, width)


def solution(mesh):
    mesh_shape = tuple(mesh.shape[axis] for axis in ("grow", "gy", "gz"))
    return jax.shard_map(
        functools.partial(on_device, mesh_shape),
        mesh=mesh,
        in_specs=(P("grow", "gy", "gz"), P(None, "grow", "gy", "gz"), P(None, "gy", "gz"), P()),
        out_specs=(P(None, "grow", "gy", "gz"), P(None, "grow", "gy", "gz")),
        check_vma=False,
    )
```

```python
import functools

import jax
import jax.numpy as jnp
from jax import lax
from jax.experimental import pallas as pl
from jax.experimental.pallas import tpu as pltpu
from jax.sharding import PartitionSpec as P

STEPS_BEFORE = 3
STEPS_AFTER = 2
STEPS = STEPS_BEFORE + STEPS_AFTER
HALF = 7
WIDE = 2 * HALF
MESH = pl.DeviceIdType.MESH


class Plan:
    def __init__(self, planes, rows, shift):
        self.planes, self.rows, self.shift = planes, rows, shift
        self.skip = (shift - STEPS) // 8 * 8
        self.own = planes - self.skip
        self.above = shift + STEPS
        self.upper = -(-self.above // 8) * 8
        self.deep = self.own + self.upper
        self.first = shift - self.skip
        self.start = self.first - STEPS + 1
        self.tiles = -(-(planes + 2 * (STEPS - 1)) // 8)
        self.tall = rows + 2 * STEPS
        self.slots = self.tall // 2


def gather_kernel(plan, mesh_shape, levels, lab, pot, codes, table, main, strip, pack, lab_up, pot_up, g_send, g_recv, y_send, y_recv, z_send, z_recv):
    g, y, z = lax.axis_index("grow"), lax.axis_index("gy"), lax.axis_index("gz")
    count_g, count_y, count_z = mesh_shape
    rows, own, tall = plan.rows, plan.own, plan.tall
    has_below, has_above = g > 0, g < count_g - 1
    y_up, y_down = lax.rem(y + 1, count_y), lax.rem(y + count_y - 1, count_y)
    z_other = lax.rem(z + 1, count_z)

    barrier = pltpu.get_barrier_semaphore()

    def greet(target):
        pl.semaphore_signal(barrier, inc=1, device_id=target, device_id_type=MESH)

    @pl.when(has_below)
    def _():
        greet((g - 1, y, z))

    @pl.when(has_above)
    def _():
        greet((g + 1, y, z))

    greet((g, y_up, z))
    greet((g, y_down, z))
    greet((g, y, z_other))
    pl.semaphore_wait(barrier, 3 + has_below.astype(jnp.int32) + has_above.astype(jnp.int32))

    split = (0, plan.upper // 3 // 8 * 8, plan.upper)
    pieces = [(piece, i) for i in range(3) for piece in range(2)]

    def g_copy(piece, i):
        begin, end = split[piece], min(split[piece + 1], plan.above)
        at = pl.ds(begin * rows, (end - begin) * rows)
        src, dst = (lab.at[at], lab_up.at[at]) if i == 0 else (pot.at[i - 1, at], pot_up.at[i - 1, at])
        sem = 3 * piece + i
        return pltpu.make_async_remote_copy(
            src_ref=src, dst_ref=dst, send_sem=g_send.at[sem], recv_sem=g_recv.at[sem],
            device_id=(g - 1, y, z), device_id_type=MESH)

    @pl.when(has_below)
    def _():
        for piece, i in pieces:
            g_copy(piece, i).start()

    def y_copies(part, i, low, size):
        copies = []
        for up in range(2):
            src, dst, target = (rows, 0, y_up) if up else (STEPS, STEPS + rows, y_down)
            sem = 2 * (3 * part + i) + up
            copy = pltpu.make_async_remote_copy(
                src_ref=main.at[i, pl.ds(src, STEPS), pl.ds(low, size)],
                dst_ref=main.at[i, pl.ds(dst, STEPS), pl.ds(low, size)],
                send_sem=y_send.at[sem], recv_sem=y_recv.at[sem],
                device_id=(g, target, z), device_id_type=MESH)
            copy.start()
            copies.append(copy)
        return copies

    def row_of(ref, i, row, begin, size):
        at = pl.ds(begin * rows + row, size, stride=rows)
        return ref[at].astype(jnp.float32) if i == 0 else ref[i - 1, at]

    y_sent = {}
    for i in range(3):
        for row in range(rows):
            main[i, STEPS + row, 0:own] = row_of(lab if i == 0 else pot, i, row, plan.skip, own)
        y_sent[0, i] = y_copies(0, i, 0, own)

    def z_copy(part, i, low, size):
        for copy in y_sent[part, i]:
            copy.wait_recv()
        lane = lax.broadcasted_iota(jnp.int32, (size, 128), 1)
        for parity in range(2):
            packed = jnp.zeros((size, 128), jnp.float32)
            for slot in range(plan.slots):
                turned = pltpu.roll(main[i, 2 * slot + parity, low : low + size], WIDE * slot + HALF, 1)
                packed = jnp.where((lane >= WIDE * slot) & (lane < WIDE * slot + WIDE), turned, packed)
            pack[i, parity, low : low + size] = packed
        sem = 3 * part + i
        at = (i, slice(None), pl.ds(low, size))
        copy = pltpu.make_async_remote_copy(
            src_ref=pack.at[at], dst_ref=strip.at[at], send_sem=z_send.at[sem], recv_sem=z_recv.at[sem],
            device_id=(g, y, z_other), device_id_type=MESH)
        copy.start()
        return copy

    def enter(piece, i):
        begin, end = split[piece], split[piece + 1]
        filled = min(end, plan.above)

        @pl.when(has_above)
        def _():
            g_copy(piece, i).wait_recv()
            for row in range(rows):
                main[i, STEPS + row, own + begin : own + filled] = row_of(lab_up if i == 0 else pot_up, i, row, begin, filled - begin)
                if end > filled:
                    main[i, STEPS + row, own + filled : own + end] = jnp.zeros((end - filled, 128), jnp.float32)

        @pl.when(jnp.logical_not(has_above))
        def _():
            melt_end = min(end, plan.shift)
            for row in range(rows):
                if i == 0:
                    value = jnp.full((melt_end - begin, 128), 3.0, jnp.float32)
                else:
                    code = codes[pl.ds(begin * rows + row, melt_end - begin, stride=rows)]
                    value = jnp.zeros((melt_end - begin, 128), jnp.float32)
                    for level in range(levels):
                        value = jnp.where(code == level, table[i - 1, level], value)
                main[i, STEPS + row, own + begin : own + melt_end] = value
                if end > melt_end:
                    main[i, STEPS + row, own + melt_end : own + end] = jnp.zeros((end - melt_end, 128), jnp.float32)

        y_sent[1 + piece, i] = y_copies(1 + piece, i, own + begin, end - begin)

    z_sent = []
    for i in range(3):
        enter(0, i)
        enter(1, i)
        z_sent.append(z_copy(0, i, 0, own))
    for piece, i in pieces:
        z_sent.append(z_copy(1 + piece, i, own + split[piece], split[piece + 1] - split[piece]))

    for copy in z_sent:
        copy.wait()
    for copies in y_sent.values():
        for copy in copies:
            copy.wait_send()

    @pl.when(has_below)
    def _():
        for piece, i in pieces:
            g_copy(piece, i).wait_send()


def cell_step(center, sums):
    p, (m0, m1) = center[:4], center[4:]
    around = sums[:3] + [6.0 - (sums[0] + sums[1] + sums[2])]
    third = 0.3 * (m0 + m1) + 0.15
    minus_w = (third + 2.1 * m0, third + 2.1 * m1, third, 3.5 * third - 0.525)
    squares = [v * v for v in p]
    shared = 0.28 - 0.6 * ((squares[0] + squares[1]) + (squares[2] + squares[3]))
    local = [p[a] * ((shared + minus_w[a]) + p[a] * (0.6 * p[a] - minus_w[a])) for a in range(4)]
    mean = 0.25 * ((local[0] + local[1]) + (local[2] + local[3])) - 0.07
    held = [jnp.clip((0.12 * around[a] - mean) + local[a], 0.0, 1.0) for a in range(4)]
    inverse = 1.0 / ((held[0] + held[1]) + (held[2] + held[3]))
    new = [v * inverse for v in held]
    change = [new[a] * new[a] * (1.5 - new[a]) - squares[a] * (1.5 - p[a]) for a in range(4)]
    release = 0.2 * (change[0] + change[1] + change[2]) + 0.7 * change[3]
    mobility = 0.0075 + 0.1425 * p[3]
    new0 = (m0 + mobility * (sums[3] - 6.0 * m0)) - (release + 1.4 * change[0])
    new1 = (m1 + mobility * (sums[4] - 6.0 * m1)) - (release + 1.4 * change[1])
    return new + [new0, new1]


def steps_kernel(plan, count_g, main0, strip0, edge0, phases, potentials, main_a, main_b, strip_a, strip_b, edges):
    g = lax.axis_index("grow")
    is_first, is_last = g == 0, g == count_g - 1
    rows, tall, deep = plan.rows, plan.tall, plan.deep

    def unpack(source, target, index):
        label = source[(0,) + index]
        for a in range(4):
            target[(a,) + index] = jnp.where(label == float(a), 1.0, 0.0)
        for i in range(2):
            target[(4 + i,) + index] = source[(1 + i,) + index]

    def unpack_row(row, carry):
        unpack(main0, main_a, (row,))
        return carry

    lax.fori_loop(0, tall, unpack_row, 0)
    for parity in range(2):
        unpack(strip0, strip_a, (parity,))
        unpack(edge0, edges, (parity,))

    lane = lax.broadcasted_iota(jnp.int32, (8, 128), 1)
    place = lax.broadcasted_iota(jnp.int32, (8, 128), 0)
    at_left, at_right = lane == 0, lane == 127
    inner_left, inner_right = lane % WIDE == HALF - 1, lane % WIDE == HALF

    def grow_sides(ref, index, low, center, top, bottom):
        above = ref[index + (pl.ds(low + 1, 8), slice(None))]
        below = ref[index + (pl.ds(low - 1, 8), slice(None))]
        if top is not None and low <= top < low + 8:
            above = jnp.where((place == top - low) & is_last, center, above)
        if bottom is not None and low <= bottom < low + 8:
            below = jnp.where((place == bottom - low) & is_first, center, below)
        return above + below

    moving = (0, 1, 2, 4, 5)

    def main_tile(src, strips, row, parity, slot, low, top, bottom):
        turn = 128 - (WIDE * slot + HALF)
        center = [src[f, row, pl.ds(low, 8), :] for f in range(6)]
        sums = []
        for f in moving:
            v = center[f]
            near = pltpu.roll(strips[f, parity, pl.ds(low, 8), :], turn, 1)
            right = pltpu.roll(jnp.where(at_left, near, v), 127, 1)
            left = pltpu.roll(jnp.where(at_right, near, v), 1, 1)
            total = grow_sides(src, (f, row), low, v, top, bottom)
            total = total + (src[f, row + 1, pl.ds(low, 8), :] + src[f, row - 1, pl.ds(low, 8), :])
            sums.append(total + (right + left))
        return cell_step(center, sums)

    def strip_tile(strips, parity, low, top, bottom):
        center = [strips[f, parity, pl.ds(low, 8), :] for f in range(6)]
        sums = []
        for f in moving:
            v = center[f]
            edge = edges[f, parity, pl.ds(low, 8), :]
            right = pltpu.roll(jnp.where(inner_right, edge, v), 127, 1)
            left = pltpu.roll(jnp.where(inner_left, edge, v), 1, 1)
            other = strips[f, 1 - parity, pl.ds(low, 8), :]
            across = pltpu.roll(other, WIDE if parity == 0 else 128 - WIDE, 1)
            total = grow_sides(strips, (f, parity), low, v, top, bottom)
            sums.append(total + (other + across) + (right + left))
        return cell_step(center, sums)

    state = (main_a, strip_a, main_b, strip_b)
    for step in range(1, STEPS + 1):
        src, strips, dst, strips_dst = state
        early = step <= STEPS_BEFORE
        top = plan.own - 1 if early else plan.first + plan.planes - 1
        bottom = None if early else plan.first
        if step < STEPS:
            for tile in range(plan.tiles):
                for parity in range(2):
                    low = plan.start + 8 * tile
                    new = strip_tile(strips, parity, low, top, bottom)
                    for f in range(6):
                        strips_dst[f, parity, pl.ds(low, 8), :] = new[f]

            count = tall - 2 * step
            group = 4 if count % 4 == 0 else 2

            def pair_step(pair, carry, step=step, group=group):
                for part in range(group):
                    row, parity = group * pair + step + part, (step + part) % 2
                    slot = group // 2 * pair + (step + part) // 2
                    turn = WIDE * slot + HALF
                    inside = (lane == turn) | (lane == turn - 1)
                    for tile in range(plan.tiles):
                        low = plan.start + 8 * tile
                        new = main_tile(src, strips, row, parity, slot, low, top, bottom)
                        for f in range(6):
                            dst[f, row, pl.ds(low, 8), :] = new[f]
                            if f in moving and step < STEPS - 1:
                                at = (f, parity, pl.ds(low, 8), slice(None))
                                edges[at] = jnp.where(inside, pltpu.roll(new[f], turn, 1), edges[at])
                return carry

            lax.fori_loop(0, count // group, pair_step, 0)
        else:
            def pair_last(pair, carry):
                for part in range(2):
                    row, parity = 2 * pair + part, (STEPS + part) % 2
                    slot = pair + (STEPS + part) // 2
                    for tile in range(plan.planes // 8):
                        low = plan.first + 8 * tile
                        new = main_tile(src, strips, row + STEPS, parity, slot, low, top, bottom)
                        at = pl.ds(8 * tile * rows + row, 8, stride=rows)
                        for f in range(4):
                            phases[f, at, :] = new[f]
                        for i in range(2):
                            potentials[i, at, :] = new[4 + i]
                return carry

            lax.fori_loop(0, rows // 2, pair_last, 0)
        if step == STEPS_BEFORE:
            melt = (slice(plan.own, plan.own + plan.shift), slice(None))

            @pl.when(is_last)
            def _():
                def fill(row, carry):
                    unpack(main0, dst, (row,) + melt)
                    return carry

                lax.fori_loop(0, tall, fill, 0)
                for parity in range(2):
                    unpack(strip0, strips_dst, (parity,) + melt)
                    unpack(edge0, edges, (parity,) + melt)

        state = (dst, strips_dst, src, strips)


def on_device(mesh_shape, labels, potential, melt_codes, melt_table):
    planes, rows, width = labels.shape
    shift, levels = melt_codes.shape[0], melt_table.shape[1]
    plan = Plan(planes, rows, shift)
    flat = planes * rows
    vmem = pl.BlockSpec(memory_space=pltpu.VMEM)
    smem = pl.BlockSpec(memory_space=pltpu.SMEM)
    f32 = jnp.float32
    dma = pltpu.SemaphoreType.DMA
    main0, strip0, edge0 = pl.pallas_call(
        functools.partial(gather_kernel, plan, mesh_shape, levels),
        out_shape=(
            pltpu.VMEM((3, plan.tall, plan.deep, width), f32),
            pltpu.VMEM((3, 2, plan.deep, width), f32),
            pltpu.VMEM((3, 2, plan.deep, width), f32),
        ),
        in_specs=[vmem, vmem, vmem, smem],
        out_specs=(vmem, vmem, vmem),
        scratch_shapes=[
            pltpu.VMEM((plan.above * rows, width), jnp.int32),
            pltpu.VMEM((2, plan.above * rows, width), f32),
            dma((6,)), dma((6,)), dma((18,)), dma((18,)), dma((9,)), dma((9,)),
        ],
        compiler_params=pltpu.CompilerParams(collective_id=0, has_side_effects=True),
        name="gather",
    )(labels.reshape(flat, width), potential.reshape(2, flat, width), melt_codes.reshape(shift * rows, width), melt_table)
    main0, strip0, edge0 = (pltpu.with_memory_space_constraint(v, pltpu.VMEM) for v in (main0, strip0, edge0))
    phases, potentials = pl.pallas_call(
        functools.partial(steps_kernel, plan, mesh_shape[0]),
        out_shape=(
            jax.ShapeDtypeStruct((4, flat, width), f32),
            jax.ShapeDtypeStruct((2, flat, width), f32),
        ),
        in_specs=[vmem, vmem, vmem],
        out_specs=(vmem, vmem),
        scratch_shapes=[
            pltpu.VMEM((6, plan.tall, plan.deep, width), f32),
            pltpu.VMEM((6, plan.tall, plan.deep, width), f32),
            pltpu.VMEM((6, 2, plan.deep, width), f32),
            pltpu.VMEM((6, 2, plan.deep, width), f32),
            pltpu.VMEM((6, 2, plan.deep, width), f32),
        ],
        name="steps",
    )(main0, strip0, edge0)
    return phases.reshape(4, planes, rows, width), potentials.reshape(2, planes, rows, width)


def solution(mesh):
    mesh_shape = tuple(mesh.shape[axis] for axis in ("grow", "gy", "gz"))
    return jax.shard_map(
        functools.partial(on_device, mesh_shape),
        mesh=mesh,
        in_specs=(P("grow", "gy", "gz"), P(None, "grow", "gy", "gz"), P(None, "gy", "gz"), P()),
        out_specs=(P(None, "grow", "gy", "gz"), P(None, "grow", "gy", "gz")),
        check_vma=False,
    )
```
